256 devices in a mesh: wide: 16 (over z_hi, x, core), col: 16 (over y, z_lo).
Axes of the slice: x: 4, y: 4, z: 8 (z_hi: 2, z_lo: 4; z = z_hi * 4 + z_lo), core: 2. Of those that a mesh axis runs over, the one named last changes fastest.
Arguments:
- adjoint: bfloat16 [32, 6144], P(None, ('wide', 'col')), may hold values from -6 to 6
- operator: bfloat16 [6144, 196608], P('wide', 'col'), may hold values from -0.109375 to 0.109375
- owner: int32 [196608], P(('col', 'wide')), may hold values from 0 to 196607, as said below
Outputs:
- junction_sums: float32 [32, 196608], P(None, ('col', 'wide'))
The draws below stay inside these ranges and needn't reach their ends.
Inputs may be any that keep to these rules, and one draw needn't show every extreme that they name: Unknown j of device block b = j // 768 (blocks ordered col first, then wide) has owner j itself, or is a duplicate whose owner is an unknown in the lower half of a block of the same index of col; duplicates lie only in the upper half of a block and owners of duplicates are never duplicates. One block hands at most 16 duplicates to the blocks of any one index of wide, and this count is reached in every draw, by some block towards every index of wide and towards some index of wide from every block.
All inputs are finite; a program needn't handle non-finite values.
Results may differ from the reference program's by a relative error of at most 0.0003.
Values may be sent and summed in bfloat16 or wider, within the bound.
No kernel may reach another device: no remote copies, remote signals or barrier semaphores. Data moves between devices by JAX's collectives and lax.ppermute only.
A program may use at most 64 MiB of HBM per device.

```python
import jax
import jax.numpy as jnp
from jax import lax

N = 196608
NRHS = 32
RD = 384
CAP = 16
ROWS = 6144
PIECE = 768
N_WIDE = 16
N_COL = 16


def draw_owner(key, part):
    wide_count = N_WIDE
    col_count = N_COL
    half_piece = PIECE // 2
    key_heavy, key_recv, key_counts, key_target, key_perm = jax.random.split(key, 5)
    heavy_send = jax.random.randint(key_heavy, (col_count,), 0, wide_count)
    heavy_recv = jax.random.randint(key_recv, (col_count,), 0, wide_count)
    counts = jax.random.randint(key_counts, (col_count, wide_count, wide_count), CAP // 4, CAP + 1)
    peers = jnp.arange(wide_count, dtype=jnp.int32)
    send_mask = peers[None, :] == heavy_send[:, None]
    recv_mask = peers[None, :] == heavy_recv[:, None]
    counts = jnp.where(send_mask[:, :, None], CAP, counts)
    counts = jnp.where(recv_mask[:, None, :], CAP, counts)
    ends = jnp.cumsum(counts, axis=2)
    starts = ends - counts
    slots = jnp.arange(half_piece, dtype=jnp.int32)
    inside = (slots[None, None, None, :] >= starts[..., None]) & (slots[None, None, None, :] < ends[..., None])
    inside_int = inside.astype(jnp.int32)
    repeated = jnp.sum(inside_int, axis=2) > 0
    target_peer = jnp.sum(inside_int * peers[None, None, :, None], axis=2)
    targets = jax.random.randint(key_target, (col_count, wide_count, half_piece), 0, half_piece)
    col_base = (jnp.arange(col_count, dtype=jnp.int32) * (wide_count * PIECE))[:, None, None]
    wide_base = (peers * PIECE)[None, :, None]
    perm_keys = jax.random.split(key_perm, col_count * wide_count)
    perms = jax.vmap(lambda k: jax.random.permutation(k, half_piece))(perm_keys).astype(jnp.int32)
    perms = perms.reshape(col_count, wide_count, half_piece)
    self_cols = col_base + wide_base + half_piece + perms
    values = jnp.where(repeated, col_base + target_peer * PIECE + targets, self_cols)

    def place(order, vals):
        return jnp.zeros((half_piece,), jnp.int32).at[order].set(vals)
    upper = jax.vmap(place)(perms.reshape(-1, half_piece), values.reshape(-1, half_piece))
    upper = upper.reshape(col_count, wide_count, half_piece)
    lower = col_base + wide_base + slots[None, None, :]
    lower = jnp.broadcast_to(lower, (col_count, wide_count, half_piece))
    return jnp.concatenate([lower, upper], axis=2).reshape(-1).astype(jnp.int32)


def with_spikes(values, rng, source, target, blocks, factor):
    owner, partner = [(jnp.arange(values.shape[axis_at]) // (values.shape[axis_at] // blocks)).reshape([-1 if axis == axis_at else 1 for axis in range(values.ndim)]) for axis_at in (source, target)]
    chosen = jax.random.permutation(rng, blocks)[partner]
    strong = (owner == chosen) | (owner == (partner + blocks // 2) % blocks)
    return jnp.where(strong, factor * values, values)


def level_of(key, extent, pieces, least, largest):
    def one(position, blocks):
        draws = jax.random.uniform(jax.random.fold_in(jax.random.fold_in(key, 6), position), (blocks,), jnp.float32, least / len(pieces), largest / len(pieces))
        return jnp.repeat(jnp.exp(draws), extent[position] // blocks).reshape((-1,) + (1,) * (len(extent) - position - 1))

    level = one(*pieces[0])
    for cut in pieces[1:]:
        level = level * one(*cut)
    return level


def bell_draw(rng, dims, scale, most, shards=(), kind=jnp.bfloat16):
    level = level_of(rng, dims, shards, -0.22, 0.18) if shards else 1.0
    entries = jax.random.normal(rng, dims, jnp.float32) * scale * level
    return jnp.minimum(jnp.maximum(entries, -most), most).astype(kind)


def gaussian_with(key, shape, deviation, reach, cuts, heavy, kind=jnp.bfloat16):
    result = deviation * jax.random.normal(key, shape, jnp.float32)
    if cuts:
        result = result * level_of(key, shape, cuts, -0.22, 0.18)
    return jnp.clip(with_spikes(result, jax.random.fold_in(key, 3), *heavy), -reach, reach).astype(kind)


def setup_inputs(seed: int = 0) -> dict:
    key_of = jax.random.split(jax.random.key(seed), 4)
    return {
        "adjoint": bell_draw(key_of[0], (NRHS, ROWS), 1.0, 6.0, ((1, 256),)),
        "operator": gaussian_with(key_of[1], (ROWS, N), ROWS ** -0.5, 0.109375, ((0, 16), (1, 16)), (0, 1, 16, 2.0)),
        "owner": draw_owner(jax.random.fold_in(key_of[3], 71), 0),
    }


def reference(adjoint, operator, owner):
    block_rows = RD
    count = ROWS // block_rows

    def accumulate(carry, index):
        start = (index * block_rows).astype(jnp.int32)
        rows_x = lax.dynamic_slice_in_dim(adjoint, start, block_rows, 1)
        rows_a = lax.dynamic_slice_in_dim(operator, start, block_rows, 0)
        return carry + jnp.dot(rows_x, rows_a, preferred_element_type=jnp.float32), None

    partials, unused = lax.scan(accumulate, jnp.zeros((NRHS, N), jnp.float32), jnp.arange(count, dtype=jnp.int32))
    summed = jax.ops.segment_sum(partials.T, owner, num_segments=N)
    return summed.T
```

```python
import functools

import jax
import jax.numpy as jnp
from jax import lax
from jax.experimental import pallas as pl
from jax.experimental.pallas import tpu as pltpu
from jax.sharding import PartitionSpec as P

CAP = 16
F32 = jnp.float32


def product_kernel(blocks, width, me_ref, adj_ref, op_ref, out_ref, buf, sems):
    me = me_ref[0]

    def copy(j):
        start = pl.multiple_of((j ^ me) * width, width)
        return pltpu.make_async_copy(op_ref.at[:, pl.ds(start, width)], buf.at[j], sems.at[j])

    for j in range(blocks):
        copy(j).start()
    adj = adj_ref[...].astype(F32).T.astype(jnp.bfloat16)
    for j in range(blocks):
        copy(j).wait()
        out_ref[j] = jnp.dot(adj, buf[j], preferred_element_type=F32)


def product(me, adj_t, operator, blocks):
    depth, cols = operator.shape
    sensors = adj_t.shape[1]
    width = cols // blocks
    return pl.pallas_call(
        functools.partial(product_kernel, blocks, width),
        out_shape=jax.ShapeDtypeStruct((blocks, sensors, width), F32),
        in_specs=[
            pl.BlockSpec(memory_space=pltpu.SMEM),
            pl.BlockSpec(memory_space=pltpu.VMEM),
            pl.BlockSpec(memory_space=pl.ANY),
        ],
        out_specs=pl.BlockSpec(memory_space=pltpu.VMEM),
        scratch_shapes=[
            pltpu.VMEM((blocks, depth, width), operator.dtype),
            pltpu.SemaphoreType.DMA((blocks,)),
        ],
        compiler_params=pltpu.CompilerParams(vmem_limit_bytes=24 << 20),
    )(me.reshape(1), adj_t, operator)


def swap(value, axis, mask):
    count = lax.axis_size(axis)
    return lax.ppermute(value, axis, [(i, i ^ mask) for i in range(count)])


def reduce_blocks(p):
    b = p.reshape((2, 4, 2) + p.shape[1:])
    s = b[:, :, 0] + swap(b[:, :, 1], "wide", 1)
    r1 = swap(s[0, 1:3], "wide", 2)
    r2 = swap(s[1, 2:4], "wide", 6)
    a0, a3 = s[0, 0] + r1[0], s[0, 3] + r1[1]
    c1, c0 = s[1, 1] + r2[0], s[1, 0] + r2[1]
    t1 = swap(a3, "wide", 6)
    t2 = swap(c1, "wide", 2)
    z = swap(c0 + t2, "wide", 8)
    return a0 + t1 + z


def local(adjoint, operator, owner):
    wide_count = lax.axis_size("wide")
    col_count = lax.axis_size("col")
    me = lax.axis_index("wide")
    own_width = owner.shape[0]
    block_cols = operator.shape[1]
    sensors = adjoint.shape[0]
    adj_t = adjoint.T
    spread = jnp.broadcast_to(adj_t[None], (col_count,) + adj_t.shape)
    adj_all = lax.all_to_all(spread, "col", split_axis=0, concat_axis=0, tiled=True)
    adj_all = adj_all.reshape(operator.shape[0], sensors)
    summed = reduce_blocks(product(me, adj_all, operator, wide_count))

    positions = jnp.arange(own_width, dtype=jnp.int32)
    global_cols = lax.axis_index("col") * block_cols + me * own_width + positions
    repeated = owner != global_cols
    target_peer = owner // own_width % wide_count
    target_place = owner % own_width
    peers = jnp.arange(wide_count, dtype=jnp.int32)
    marks = ((target_peer[:, None] == peers[None, :]) & repeated[:, None]).astype(jnp.int32)
    ranking = jnp.sum((jnp.cumsum(marks, axis=0) - marks) * marks, axis=1)
    slot_of = target_peer * CAP + ranking
    slot_ids = jnp.arange(wide_count * CAP, dtype=jnp.int32)
    chosen = (slot_of[:, None] == slot_ids[None, :]) & repeated[:, None]
    selector = chosen.astype(F32)
    outgoing = jnp.dot(summed, selector, precision=lax.Precision.HIGHEST, preferred_element_type=F32)
    place_sum = jnp.sum(chosen.astype(jnp.int32) * (target_place + 1)[:, None], axis=0) - 1
    outgoing = outgoing.reshape(sensors, wide_count, CAP)
    places = place_sum.astype(F32).reshape(1, wide_count, CAP)
    packed = jnp.concatenate([outgoing, jnp.broadcast_to(places, (8, wide_count, CAP))], axis=0)
    arrived = lax.all_to_all(packed, "wide", split_axis=1, concat_axis=1, tiled=True)
    flat_values = arrived[:sensors].reshape(sensors, wide_count * CAP)
    landing = arrived[sensors].reshape(-1).astype(jnp.int32)
    receiver = (landing[:, None] == positions[None, :]).astype(F32)
    kept = jnp.where(repeated[None, :], 0.0, summed)
    added = jnp.dot(flat_values, receiver, precision=lax.Precision.HIGHEST, preferred_element_type=F32)
    return kept + added


def solution(mesh):
    return jax.shard_map(
        local,
        mesh=mesh,
        in_specs=(P(None, ("wide", "col")), P("wide", "col"), P(("col", "wide"))),
        out_specs=P(None, ("col", "wide")),
        check_vma=False,
    )
```

```python
import functools

import jax
import jax.numpy as jnp
from jax import lax
from jax.experimental import pallas as pl
from jax.experimental.pallas import tpu as pltpu
from jax.sharding import PartitionSpec as P


CAP = 16
F32, BF16, I32 = jnp.float32, jnp.bfloat16, jnp.int32
VMEM = pl.BlockSpec(memory_space=pltpu.VMEM)
HBM = pl.BlockSpec(memory_space=pltpu.HBM)
COL_MASKS = (4, 12, 1, 2)
WIDE_MASKS = (1, 2, 6, 8)
GROUP = 4


def doubling_order(masks):
    order = [0]
    for mask in masks:
        order += [i ^ mask for i in order]
    return tuple(order)


def swap(value, axis, mask):
    count = lax.axis_size(axis)
    return lax.ppermute(value, axis, [(i, i ^ mask) for i in range(count)])


def prepare_kernel(peers, owner_hbm, adj_hbm, rows_ref, out_ref, owner_ref, sems):
    copies = [
        pltpu.make_async_copy(owner_hbm, owner_ref, sems.at[0]),
        pltpu.make_async_copy(adj_hbm, rows_ref, sems.at[1]),
    ]
    for copy in copies:
        copy.start()
    for copy in copies:
        copy.wait()
    lines, lane = owner_ref.shape
    width = lines * lane
    half = width // 2
    first = lax.axis_index("col") * (peers * width)
    parts = [owner_ref[i : i + 1] for i in range(lines // 2, lines)]
    owner = jnp.concatenate(parts, axis=1) - first
    own = lax.broadcasted_iota(I32, (1, half), 1) + (lax.axis_index("wide") * width + half)
    repeated = owner != own
    peer = owner // width
    place = owner - peer * width
    ids = lax.broadcasted_iota(I32, (peers, half), 0)
    marks = jnp.where((ids == peer) & repeated, 1.0, 0.0)
    rows = lax.broadcasted_iota(I32, (half, half), 0)
    columns = lax.broadcasted_iota(I32, (half, half), 1)
    earlier = jnp.where(rows < columns, 1.0, 0.0).astype(BF16)
    ahead = jnp.dot(marks.astype(BF16), earlier, preferred_element_type=F32)
    rank = jnp.sum(ahead * marks, axis=0, keepdims=True).astype(I32)
    out_ref[0, 0:1] = jnp.where(repeated, peer * CAP + rank, -1)
    out_ref[0, 1:2] = place_code(place)


def place_code(place):
    return jnp.where(place < 255, place + 1, 254 - place)


def adjoint_rows(order, pieces, rows_ref):
    me = lax.axis_index("col")
    depth, n = pieces[0].shape
    blocks = [piece[i : i + depth] for piece in pieces for i in range(0, piece.shape[0], depth)]
    for block, offset in zip(blocks, order):
        start = pl.multiple_of((me ^ offset) * depth, 8)
        rows_ref[pl.ds(start, depth), 0:n] = block.astype(F32)
    return rows_ref[:, 0:n].T.astype(BF16)


def operator_copies(targets, shift, op_ref, buf, sems):
    me = lax.axis_index("wide")
    half = buf.shape[2]

    def copy(i):
        start = pl.multiple_of((targets[i] ^ me) * (2 * half) + shift, 128)
        return pltpu.make_async_copy(op_ref.at[:, pl.ds(start, half)], buf.at[i], sems.at[i])

    for i in range(len(targets)):
        copy(i).start()
    return copy


def upper_kernel(blocks, order, *refs):
    *pieces, op_ref, keep_ref, send_ref, buf, rows_ref, sems = refs
    copy = operator_copies(range(blocks), buf.shape[2], op_ref, buf, sems)

    @pl.when(lax.axis_index("wide") >= 0)
    def _():
        adj = adjoint_rows(order, pieces, rows_ref)
        for first in range(0, blocks, GROUP):
            for j in range(first, first + GROUP):
                copy(j).wait()
            for j in range(first, first + GROUP):
                out = send_ref if j % 2 else keep_ref
                out[j // 2] = jnp.dot(adj, buf[j], preferred_element_type=F32)


def lower_blocks(targets, adj, slots, buf, keep_ref, send_ref):
    n = adj.shape[0]
    total, half = slots.shape[1], buf.shape[2]
    lanes = place_code(lax.broadcasted_iota(I32, (total, half), 1)).astype(F32).astype(BF16)
    for i in range(len(targets)):
        filled = slots[i]
        place = filled[:, 2 * n : 2 * n + 1]
        land = jnp.where(lanes == place, jnp.bfloat16(1), jnp.bfloat16(0))
        added = lax.dot_general(
            filled[:, 0 : 2 * n], land, (((0,), (0,)), ((), ())), preferred_element_type=F32
        )
        out = send_ref if i % 2 else keep_ref
        base = jnp.dot(adj, buf[i], preferred_element_type=F32)
        out[i // 2] = base + (added[0:n] + added[n : 2 * n])


def far_kernel(blocks, order, slot_order, codes_ref, up_keep_ref, up_send_ref, *refs):
    *pieces, op_ref, keep_ref, send_ref, near_slots, buf, rows_ref, slots, sems = refs
    targets = range(blocks // 2, blocks)
    copy = operator_copies(targets, 0, op_ref, buf, sems)
    half = buf.shape[2]
    n = up_keep_ref.shape[1]
    total = blocks * CAP

    @pl.when(lax.axis_index("wide") >= 0)
    def _():
        mine = lax.axis_index("wide") * CAP
        adj = adjoint_rows(order, pieces, rows_ref)
        ids = lax.broadcasted_iota(I32, (total, half), 0)
        for i, j in enumerate(slot_order):
            code = codes_ref[i]
            slot = jnp.where(code[0:1] < 0, -1, code[0:1] ^ mine)
            pick = jnp.where(ids == slot, 1.0, 0.0).astype(BF16)
            value = (up_send_ref if j % 2 else up_keep_ref)[j // 2]
            high = value.astype(BF16)
            low = (value - high.astype(F32)).astype(BF16)
            place = jnp.broadcast_to(code[1:2], (16, half)).astype(F32).astype(BF16)
            data = jnp.concatenate([high, low, place], axis=0)
            got = lax.dot_general(pick, data, (((1,), (1,)), ((), ())), preferred_element_type=F32)
            got = got.astype(BF16).reshape(blocks, CAP, 2 * n + 16)
            near_slots[:, j * CAP : (j + 1) * CAP, 0 : 2 * n + 16] = got[: blocks // 2]
            slots[:, j * CAP : (j + 1) * CAP, 0 : 2 * n + 16] = got[blocks // 2 :]
        for i in range(len(targets)):
            copy(i).wait()
        lower_blocks(targets, adj, slots, buf, keep_ref, send_ref)


def near_kernel(blocks, order, slots, *refs):
    *pieces, op_ref, keep_ref, send_ref, buf, rows_ref, sems = refs
    targets = range(blocks // 2)
    copy = operator_copies(targets, 0, op_ref, buf, sems)

    @pl.when(lax.axis_index("wide") >= 0)
    def _():
        adj = adjoint_rows(order, pieces, rows_ref)
        for i in range(len(targets)):
            copy(i).wait()
        lower_blocks(targets, adj, slots, buf, keep_ref, send_ref)


def half_products(kernel, count, operator, operands, half, extra=(), scratch=()):
    depth = operator.shape[0]
    n = operands[-1].shape[1]
    operator = pltpu.with_memory_space_constraint(operator, pltpu.HBM)
    shape = jax.ShapeDtypeStruct((count // 2, n, half), F32)
    return pl.pallas_call(
        kernel,
        out_shape=(shape, shape, *extra),
        in_specs=[VMEM] * len(operands) + [HBM],
        out_specs=(VMEM,) * (2 + len(extra)),
        scratch_shapes=[
            pltpu.VMEM((count, depth, half), operator.dtype),
            pltpu.VMEM((depth, 128), F32),
            *scratch,
            pltpu.SemaphoreType.DMA((count,)),
        ],
        compiler_params=pltpu.CompilerParams(vmem_limit_bytes=24 << 20),
    )(*operands, operator)


def program(adjoint, operator, owner):
    blocks = lax.axis_size("wide")
    lines = owner.shape[0] // 128
    half = owner.shape[0] // 2
    adj_t = adjoint.T
    rows, codes = pl.pallas_call(
        functools.partial(prepare_kernel, blocks),
        out_shape=(
            jax.ShapeDtypeStruct(adj_t.shape, adj_t.dtype),
            jax.ShapeDtypeStruct((1, 2, half), I32),
        ),
        in_specs=[HBM, HBM],
        out_specs=(VMEM, VMEM),
        scratch_shapes=[pltpu.VMEM((lines, 128), I32), pltpu.SemaphoreType.DMA((2,))],
        compiler_params=pltpu.CompilerParams(vmem_limit_bytes=4 << 20),
        name="prepare",
    )(
        pltpu.with_memory_space_constraint(owner.reshape(lines, 128), pltpu.HBM),
        pltpu.with_memory_space_constraint(adj_t, pltpu.HBM),
    )
    code = codes[0]
    pieces = [rows]
    for col_mask, wide_mask in zip(COL_MASKS, WIDE_MASKS):
        pieces.append(swap(jnp.concatenate(pieces, axis=0), "col", col_mask))
        codes_in = swap(codes, "wide", wide_mask)
        codes = jnp.concatenate([codes, codes_in], axis=0)
    order, slot_order = doubling_order(COL_MASKS), doubling_order(WIDE_MASKS)
    up_keep, up_send = half_products(
        functools.partial(upper_kernel, blocks, order), blocks, operator, pieces, half
    )
    slots = (blocks // 2, blocks * CAP, 128)
    far_keep, far_send, near_slots = half_products(
        functools.partial(far_kernel, blocks, order, slot_order),
        blocks // 2,
        operator,
        [codes, up_keep, up_send] + pieces,
        half,
        (jax.ShapeDtypeStruct(slots, BF16),),
        (pltpu.VMEM(slots, BF16),),
    )
    near_keep, near_send = half_products(
        functools.partial(near_kernel, blocks, order),
        blocks // 2,
        operator,
        [near_slots] + pieces,
        half,
    )
    upper = up_keep + swap(up_send, "wide", 1)
    far = far_keep + swap(far_send, "wide", 1)
    near = near_keep + swap(near_send, "wide", 1)
    far = jnp.stack([far, upper[4:]], axis=1)
    near = jnp.stack([near, upper[:4]], axis=1)
    r2 = swap(far[2:4], "wide", 6)
    t2 = swap(far[1] + r2[0], "wide", 2)
    across = swap(far[0] + r2[1] + t2, "wide", 8)
    r1 = swap(near[2:4], "wide", 6)
    t1 = swap(near[1] + r1[0], "wide", 2)
    total = near[0] + r1[1] + t1 + across
    return jnp.concatenate([total[0], jnp.where(code[0:1] >= 0, 0.0, total[1])], axis=1)


def solution(mesh):
    return jax.shard_map(
        program,
        mesh=mesh,
        in_specs=(P(None, ("wide", "col")), P("wide", "col"), P(("col", "wide"))),
        out_specs=P(None, ("col", "wide")),
        check_vma=False,
    )
```

```python
import functools

import jax
import jax.numpy as jnp
from jax import lax
from jax.experimental import pallas as pl
from jax.experimental.pallas import tpu as pltpu
from jax.sharding import PartitionSpec as P


CAP = 16
F32, BF16, I32 = jnp.float32, jnp.bfloat16, jnp.int32
VMEM = pl.BlockSpec(memory_space=pltpu.VMEM)
HBM = pl.BlockSpec(memory_space=pltpu.HBM)
COL_MASKS = (4, 12, 1, 2)
WIDE_MASKS = (1, 2, 6, 8)
GROUP = 4
LEVEL = 14.0


def doubling_order(masks):
    order = [0]
    for mask in masks:
        order += [i ^ mask for i in order]
    return tuple(order)


def swap(value, axis, mask):
    count = lax.axis_size(axis)
    return lax.ppermute(value, axis, [(i, i ^ mask) for i in range(count)])


def prepare_kernel(peers, owner_hbm, adj_hbm, rows_ref, out_ref, owner_ref, sems):
    copies = [
        pltpu.make_async_copy(owner_hbm, owner_ref, sems.at[0]),
        pltpu.make_async_copy(adj_hbm, rows_ref, sems.at[1]),
    ]
    for copy in copies:
        copy.start()
    for copy in copies:
        copy.wait()
    lines, lane = owner_ref.shape
    width = lines * lane
    half = width // 2
    first = lax.axis_index("col") * (peers * width)
    parts = [owner_ref[i : i + 1] for i in range(lines // 2, lines)]
    owner = jnp.concatenate(parts, axis=1) - first
    own = lax.broadcasted_iota(I32, (1, half), 1) + (lax.axis_index("wide") * width + half)
    repeated = owner != own
    peer = owner // width
    place = owner - peer * width
    ids = lax.broadcasted_iota(I32, (peers, half), 0)
    marks = jnp.where((ids == peer) & repeated, 1.0, 0.0)
    rows = lax.broadcasted_iota(I32, (half, half), 0)
    columns = lax.broadcasted_iota(I32, (half, half), 1)
    earlier = jnp.where(rows < columns, 1.0, 0.0).astype(BF16)
    ahead = jnp.dot(marks.astype(BF16), earlier, preferred_element_type=F32)
    rank = jnp.sum(ahead * marks, axis=0, keepdims=True).astype(I32)
    out_ref[0, 0:1] = jnp.where(repeated, peer * CAP + rank, -1)
    out_ref[0, 1:2] = place_code(place)


def place_code(place):
    return jnp.where(place < 255, place + 1, 254 - place)


def adjoint_rows(order, pieces, rows_ref):
    me = lax.axis_index("col")
    depth, n = pieces[0].shape
    blocks = [piece[i : i + depth] for piece in pieces for i in range(0, piece.shape[0], depth)]
    for block, offset in zip(blocks, order):
        start = pl.multiple_of((me ^ offset) * depth, 8)
        rows_ref[pl.ds(start, depth), 0:n] = block.astype(F32)
    return rows_ref[:, 0:n].T.astype(BF16)


def operator_copies(targets, shift, op_ref, buf, sems):
    me = lax.axis_index("wide")
    half = buf.shape[2]

    def copy(i):
        start = pl.multiple_of((targets[i] ^ me) * (2 * half) + shift, 128)
        return pltpu.make_async_copy(op_ref.at[:, pl.ds(start, half)], buf.at[i], sems.at[i])

    for i in range(len(targets)):
        copy(i).start()
    return copy


def upper_kernel(blocks, order, *refs):
    *pieces, op_ref, keep_ref, send_ref, buf, rows_ref, sems = refs
    copy = operator_copies(range(blocks), buf.shape[2], op_ref, buf, sems)

    @pl.when(lax.axis_index("wide") >= 0)
    def _():
        adj = adjoint_rows(order, pieces, rows_ref)
        for first in range(0, blocks, GROUP):
            for j in range(first, first + GROUP):
                copy(j).wait()
            for j in range(first, first + GROUP):
                out = send_ref if j % 2 else keep_ref
                out[j // 2] = jnp.dot(adj, buf[j], preferred_element_type=F32)


def lower_blocks(targets, adj, slots, buf, keep_ref, send_ref):
    n = adj.shape[0]
    total, half = slots.shape[1], buf.shape[2]
    lanes = place_code(lax.broadcasted_iota(I32, (total, half), 1)).astype(F32).astype(BF16)
    largest = jnp.zeros((n, half), F32)
    for i in range(len(targets)):
        filled = slots[i]
        place = filled[:, 2 * n : 2 * n + 1]
        land = jnp.where(lanes == place, jnp.bfloat16(1), jnp.bfloat16(0))
        added = lax.dot_general(
            filled[:, 0 : 2 * n], land, (((0,), (0,)), ((), ())), preferred_element_type=F32
        )
        out = send_ref if i % 2 else keep_ref
        base = jnp.dot(adj, buf[i], preferred_element_type=F32)
        value = base + (added[0:n] + added[n : 2 * n])
        out[i // 2] = value
        largest = jnp.maximum(largest, jnp.abs(value))
    return largest


def far_kernel(blocks, order, slot_order, *refs):
    count = len(WIDE_MASKS) + 1
    codes, (up_keep_ref, up_send_ref), refs = refs[:count], refs[count : count + 2], refs[count + 2 :]
    *pieces, op_ref, keep_ref, send_ref, near_slots, buf, rows_ref, slots, sems = refs
    targets = range(blocks // 2, blocks)
    copy = operator_copies(targets, 0, op_ref, buf, sems)
    half = buf.shape[2]
    n = up_keep_ref.shape[1]
    total = blocks * CAP

    @pl.when(lax.axis_index("wide") >= 0)
    def _():
        mine = lax.axis_index("wide") * CAP
        adj = adjoint_rows(order, pieces, rows_ref)
        ids = lax.broadcasted_iota(I32, (total, half), 0)
        code_rows = [ref[i] for ref in codes for i in range(ref.shape[0])]
        largest = jnp.zeros((n, half), F32)
        for code, j in zip(code_rows, slot_order):
            slot = jnp.where(code[0:1] < 0, -1, code[0:1] ^ mine)
            pick = jnp.where(ids == slot, 1.0, 0.0).astype(BF16)
            value = (up_send_ref if j % 2 else up_keep_ref)[j // 2]
            largest = jnp.maximum(largest, jnp.abs(value))
            high = value.astype(BF16)
            low = (value - high.astype(F32)).astype(BF16)
            place = jnp.broadcast_to(code[1:2], (16, half)).astype(F32).astype(BF16)
            data = jnp.concatenate([high, low, place], axis=0)
            got = lax.dot_general(pick, data, (((1,), (1,)), ((), ())), preferred_element_type=F32)
            got = got.astype(BF16).reshape(blocks, CAP, 2 * n + 16)
            near_slots[:, j * CAP : (j + 1) * CAP, 0 : 2 * n + 16] = got[: blocks // 2]
            slots[:, j * CAP : (j + 1) * CAP, 0 : 2 * n + 16] = got[blocks // 2 :]
        for i in range(len(targets)):
            copy(i).wait()
        largest = jnp.maximum(largest, lower_blocks(targets, adj, slots, buf, keep_ref, send_ref))
        largest = jnp.max(jnp.max(largest, axis=0, keepdims=True), axis=1, keepdims=True)
        level = jnp.ceil(jnp.log2(jnp.maximum(largest, 2.0**-90))) + 1.0
        send_ref[len(targets) // 2] = jnp.broadcast_to(level, (n, half))


def near_kernel(blocks, order, slots, *refs):
    *pieces, op_ref, keep_ref, send_ref, buf, rows_ref, sems = refs
    targets = range(blocks // 2)
    copy = operator_copies(targets, 0, op_ref, buf, sems)

    @pl.when(lax.axis_index("wide") >= 0)
    def _():
        adj = adjoint_rows(order, pieces, rows_ref)
        for i in range(len(targets)):
            copy(i).wait()
        lower_blocks(targets, adj, slots, buf, keep_ref, send_ref)


def half_products(kernel, count, operator, operands, half, extra=(), scratch=(), more=0):
    depth = operator.shape[0]
    n = operands[-1].shape[1]
    operator = pltpu.with_memory_space_constraint(operator, pltpu.HBM)
    shape = jax.ShapeDtypeStruct((count // 2, n, half), F32)
    return pl.pallas_call(
        kernel,
        out_shape=(shape, jax.ShapeDtypeStruct((count // 2 + more, n, half), F32), *extra),
        in_specs=[VMEM] * len(operands) + [HBM],
        out_specs=(VMEM,) * (2 + len(extra)),
        scratch_shapes=[
            pltpu.VMEM((count, depth, half), operator.dtype),
            pltpu.VMEM((depth, 128), F32),
            *scratch,
            pltpu.SemaphoreType.DMA((count,)),
        ],
        compiler_params=pltpu.CompilerParams(vmem_limit_bytes=24 << 20),
    )(*operands, operator)


def pack(value, level):
    rows = value.reshape(-1, value.shape[-1])
    scaled = (rows * jnp.exp2(LEVEL - level)).astype(jnp.float16)
    return jnp.concatenate([scaled, jnp.broadcast_to(level, (16, rows.shape[1])).astype(jnp.float16)], axis=0)


def unpack(message, shape):
    rows = message.astype(F32)
    level = rows[-1:]
    return (rows[:-16] * jnp.exp2(level - LEVEL)).reshape(shape), level


def program(adjoint, operator, owner):
    blocks = lax.axis_size("wide")
    lines = owner.shape[0] // 128
    half = owner.shape[0] // 2
    adj_t = adjoint.T
    rows, codes = pl.pallas_call(
        functools.partial(prepare_kernel, blocks),
        out_shape=(
            jax.ShapeDtypeStruct(adj_t.shape, adj_t.dtype),
            jax.ShapeDtypeStruct((1, 2, half), I32),
        ),
        in_specs=[HBM, HBM],
        out_specs=(VMEM, VMEM),
        scratch_shapes=[pltpu.VMEM((lines, 128), I32), pltpu.SemaphoreType.DMA((2,))],
        compiler_params=pltpu.CompilerParams(vmem_limit_bytes=4 << 20),
        name="prepare",
    )(
        pltpu.with_memory_space_constraint(owner.reshape(lines, 128), pltpu.HBM),
        pltpu.with_memory_space_constraint(adj_t, pltpu.HBM),
    )
    code = codes[0]
    pieces, code_pieces = [rows], [codes]
    for col_mask, wide_mask in zip(COL_MASKS, WIDE_MASKS):
        pieces.append(swap(jnp.concatenate(pieces, axis=0), "col", col_mask))
        code_pieces.append(swap(jnp.concatenate(code_pieces, axis=0), "wide", wide_mask))
    order, slot_order = doubling_order(COL_MASKS), doubling_order(WIDE_MASKS)
    up_keep, up_send = half_products(
        functools.partial(upper_kernel, blocks, order), blocks, operator, pieces, half
    )
    slots = (blocks // 2, blocks * CAP, 128)
    far_keep, far_send, near_slots = half_products(
        functools.partial(far_kernel, blocks, order, slot_order),
        blocks // 2,
        operator,
        code_pieces + [up_keep, up_send] + pieces,
        half,
        (jax.ShapeDtypeStruct(slots, BF16),),
        (pltpu.VMEM(slots, BF16),),
        more=1,
    )
    near_keep, near_send = half_products(
        functools.partial(near_kernel, blocks, order),
        blocks // 2,
        operator,
        [near_slots] + pieces,
        half,
    )
    upper = up_keep + swap(up_send, "wide", 1)
    far_in = swap(far_send, "wide", 1)
    far = far_keep + far_in[:-1]
    level = jnp.maximum(far_send[-1, 0:1], far_in[-1, 0:1]) + 1.0
    near = near_keep + swap(near_send, "wide", 1)
    far = jnp.stack([far, upper[4:]], axis=1)
    near = jnp.stack([near, upper[:4]], axis=1)
    message = swap(pack(far[2:4], level), "wide", 6)
    r2, other = unpack(message, far[2:4].shape)
    level = jnp.maximum(level, other) + 1.0
    message = swap(pack(far[1] + r2[0], level), "wide", 2)
    t2, other = unpack(message, far[1].shape)
    level = jnp.maximum(level, other) + 1.0
    message = swap(pack(far[0] + r2[1] + t2, level), "wide", 8)
    across, other = unpack(message, far[0].shape)
    r1 = swap(near[2:4], "wide", 6)
    t1 = swap(near[1] + r1[0], "wide", 2)
    total = near[0] + r1[1] + t1 + across
    return jnp.concatenate([total[0], jnp.where(code[0:1] >= 0, 0.0, total[1])], axis=1)


def solution(mesh):
    return jax.shard_map(
        program,
        mesh=mesh,
        in_specs=(P(None, ("wide", "col")), P("wide", "col"), P(("col", "wide"))),
        out_specs=P(None, ("col", "wide")),
        check_vma=False,
    )
```

```python
import functools

import jax
import jax.numpy as jnp
from jax import lax
from jax.experimental import pallas as pl
from jax.experimental.pallas import tpu as pltpu
from jax.sharding import PartitionSpec as P


CAP = 16
F32, BF16, I32 = jnp.float32, jnp.bfloat16, jnp.int32
VMEM = pl.BlockSpec(memory_space=pltpu.VMEM)
HBM = pl.BlockSpec(memory_space=pltpu.HBM)
COL_MASKS = (2, 1, 4, 12)
WIDE_MASKS = (1, 2, 6, 8)
GROUP = 4
LEVEL = 14.0


def doubling_order(masks):
    order = [0]
    for mask in masks:
        order += [i ^ mask for i in order]
    return tuple(order)


def swap(value, axis, mask):
    count = lax.axis_size(axis)
    return lax.ppermute(value, axis, [(i, i ^ mask) for i in range(count)])


def prepare_kernel(peers, owner_hbm, adj_hbm, rows_ref, out_ref, owner_ref, sems):
    copies = [
        pltpu.make_async_copy(owner_hbm, owner_ref, sems.at[0]),
        pltpu.make_async_copy(adj_hbm, rows_ref, sems.at[1]),
    ]
    for copy in copies:
        copy.start()
    for copy in copies:
        copy.wait()
    lines, lane = owner_ref.shape
    width = lines * lane
    half = width // 2
    first = lax.axis_index("col") * (peers * width)
    parts = [owner_ref[i : i + 1] for i in range(lines // 2, lines)]
    owner = jnp.concatenate(parts, axis=1) - first
    own = lax.broadcasted_iota(I32, (1, half), 1) + (lax.axis_index("wide") * width + half)
    repeated = owner != own
    peer = owner // width
    place = owner - peer * width
    ids = lax.broadcasted_iota(I32, (peers, half), 0)
    marks = jnp.where((ids == peer) & repeated, 1.0, 0.0)
    rows = lax.broadcasted_iota(I32, (half, half), 0)
    columns = lax.broadcasted_iota(I32, (half, half), 1)
    earlier = jnp.where(rows < columns, 1.0, 0.0).astype(BF16)
    ahead = jnp.dot(marks.astype(BF16), earlier, preferred_element_type=F32)
    rank = jnp.sum(ahead * marks, axis=0, keepdims=True).astype(I32)
    out_ref[0, 0:1] = jnp.where(repeated, peer * CAP + rank, -1)
    out_ref[0, 1:2] = place_code(place)


def place_code(place):
    return jnp.where(place < 255, place + 1, 254 - place)


def adjoint_rows(order, pieces, rows_ref):
    me = lax.axis_index("col")
    depth, n = pieces[0].shape
    blocks = [piece[i : i + depth] for piece in pieces for i in range(0, piece.shape[0], depth)]
    for block, offset in zip(blocks, order):
        start = pl.multiple_of((me ^ offset) * depth, 8)
        rows_ref[pl.ds(start, depth), 0:n] = block.astype(F32)
    return rows_ref[:, 0:n].T.astype(BF16)


def operator_copies(targets, shift, op_ref, buf, sems):
    me = lax.axis_index("wide")
    half = buf.shape[2]

    def copy(i):
        start = pl.multiple_of((targets[i] ^ me) * (2 * half) + shift, 128)
        return pltpu.make_async_copy(op_ref.at[:, pl.ds(start, half)], buf.at[i], sems.at[i])

    for i in range(len(targets)):
        copy(i).start()
    return copy


def upper_kernel(blocks, order, *refs):
    *pieces, op_ref, keep_ref, send_ref, adj_ref, buf, rows_ref, sems = refs
    copy = operator_copies(range(blocks), buf.shape[2], op_ref, buf, sems)

    @pl.when(lax.axis_index("wide") >= 0)
    def _():
        adj = adjoint_rows(order, pieces, rows_ref)
        adj_ref[...] = adj
        for first in range(0, blocks, GROUP):
            for j in range(first, first + GROUP):
                copy(j).wait()
            for j in range(first, first + GROUP):
                out = send_ref if j % 2 else keep_ref
                out[j // 2] = jnp.dot(adj, buf[j], preferred_element_type=F32)


def lower_blocks(copy, group, adj, slots, buf, keep_ref, send_ref):
    n = adj.shape[0]
    count = slots.shape[0]
    total, half = slots.shape[1], buf.shape[2]
    lanes = place_code(lax.broadcasted_iota(I32, (total, half), 1)).astype(F32).astype(BF16)
    largest = jnp.zeros((n, half), F32)
    for i in range(count):
        if i % group == 0:
            for arriving in range(i, i + group):
                copy(arriving).wait()
        filled = slots[i]
        place = filled[:, 2 * n : 2 * n + 1]
        land = jnp.where(lanes == place, jnp.bfloat16(1), jnp.bfloat16(0))
        added = lax.dot_general(
            filled[:, 0 : 2 * n], land, (((0,), (0,)), ((), ())), preferred_element_type=F32
        )
        out = send_ref if i % 2 else keep_ref
        base = jnp.dot(adj, buf[i], preferred_element_type=F32)
        value = base + (added[0:n] + added[n : 2 * n])
        out[i // 2] = value
        largest = jnp.maximum(largest, jnp.abs(value))
    return largest


def far_kernel(blocks, slot_order, *refs):
    count = len(WIDE_MASKS) + 1
    codes, (up_keep_ref, up_send_ref), refs = refs[:count], refs[count : count + 2], refs[count + 2 :]
    adj_ref, op_ref, keep_ref, send_ref, near_slots, buf, slots, sems = refs
    targets = range(blocks // 2, blocks)
    copy = operator_copies(targets, 0, op_ref, buf, sems)
    half = buf.shape[2]
    n = up_keep_ref.shape[1]
    total = blocks * CAP

    @pl.when(lax.axis_index("wide") >= 0)
    def _():
        mine = lax.axis_index("wide") * CAP
        adj = adj_ref[...]
        ids = lax.broadcasted_iota(I32, (total, half), 0)
        code_rows = [ref[i] for ref in codes for i in range(ref.shape[0])]
        largest = jnp.zeros((n, half), F32)
        for code, j in zip(code_rows, slot_order):
            slot = jnp.where(code[0:1] < 0, -1, code[0:1] ^ mine)
            pick = jnp.where(ids == slot, 1.0, 0.0).astype(BF16)
            value = (up_send_ref if j % 2 else up_keep_ref)[j // 2]
            largest = jnp.maximum(largest, jnp.abs(value))
            high = value.astype(BF16)
            low = (value - high.astype(F32)).astype(BF16)
            place = jnp.broadcast_to(code[1:2], (16, half)).astype(F32).astype(BF16)
            data = jnp.concatenate([high, low, place], axis=0)
            got = lax.dot_general(pick, data, (((1,), (1,)), ((), ())), preferred_element_type=F32)
            got = got.astype(BF16).reshape(blocks, CAP, 2 * n + 16)
            near_slots[:, j * CAP : (j + 1) * CAP, 0 : 2 * n + 16] = got[: blocks // 2]
            slots[:, j * CAP : (j + 1) * CAP, 0 : 2 * n + 16] = got[blocks // 2 :]
        count = len(targets)
        largest = jnp.maximum(largest, lower_blocks(copy, count, adj, slots, buf, keep_ref, send_ref))
        largest = jnp.max(jnp.max(largest, axis=0, keepdims=True), axis=1, keepdims=True)
        level = jnp.ceil(jnp.log2(jnp.maximum(largest, 2.0**-90))) + 1.0
        send_ref[len(targets) // 2] = jnp.broadcast_to(level, (n, half))


def near_kernel(blocks, slots, adj_ref, op_ref, keep_ref, send_ref, buf, sems):
    copy = operator_copies(range(blocks // 2), 0, op_ref, buf, sems)

    @pl.when(lax.axis_index("wide") >= 0)
    def _():
        lower_blocks(copy, GROUP, adj_ref[...], slots, buf, keep_ref, send_ref)


def half_products(kernel, count, operator, operands, shape, extra=(), scratch=(), more=0):
    depth = operator.shape[0]
    operator = pltpu.with_memory_space_constraint(operator, pltpu.HBM)
    n, half = shape
    keep = jax.ShapeDtypeStruct((count // 2, n, half), F32)
    send = jax.ShapeDtypeStruct((count // 2 + more, n, half), F32)
    return pl.pallas_call(
        kernel,
        out_shape=(keep, send, *extra),
        in_specs=[VMEM] * len(operands) + [HBM],
        out_specs=(VMEM,) * (2 + len(extra)),
        scratch_shapes=[
            pltpu.VMEM((count, depth, half), operator.dtype),
            *scratch,
            pltpu.SemaphoreType.DMA((count,)),
        ],
        compiler_params=pltpu.CompilerParams(vmem_limit_bytes=24 << 20),
    )(*operands, operator)


def pack(value, level):
    rows = value.reshape(-1, value.shape[-1])
    scaled = (rows * jnp.exp2(LEVEL - level)).astype(jnp.float16)
    return jnp.concatenate([scaled, jnp.broadcast_to(level, (16, rows.shape[1])).astype(jnp.float16)], axis=0)


def unpack(message, shape):
    rows = message.astype(F32)
    level = rows[-1:]
    return (rows[:-16] * jnp.exp2(level - LEVEL)).reshape(shape), level


def program(adjoint, operator, owner):
    blocks = lax.axis_size("wide")
    lines = owner.shape[0] // 128
    half = owner.shape[0] // 2
    adj_t = adjoint.T
    rows, codes = pl.pallas_call(
        functools.partial(prepare_kernel, blocks),
        out_shape=(
            jax.ShapeDtypeStruct(adj_t.shape, adj_t.dtype),
            jax.ShapeDtypeStruct((1, 2, half), I32),
        ),
        in_specs=[HBM, HBM],
        out_specs=(VMEM, VMEM),
        scratch_shapes=[pltpu.VMEM((lines, 128), I32), pltpu.SemaphoreType.DMA((2,))],
        compiler_params=pltpu.CompilerParams(vmem_limit_bytes=4 << 20),
        name="prepare",
    )(
        pltpu.with_memory_space_constraint(owner.reshape(lines, 128), pltpu.HBM),
        pltpu.with_memory_space_constraint(adj_t, pltpu.HBM),
    )
    code = codes[0]
    pieces, code_pieces = [rows], [codes]
    for col_mask, wide_mask in zip(COL_MASKS, WIDE_MASKS):
        pieces.append(swap(jnp.concatenate(pieces, axis=0), "col", col_mask))
        code_pieces.append(swap(jnp.concatenate(code_pieces, axis=0), "wide", wide_mask))
    order, slot_order = doubling_order(COL_MASKS), doubling_order(WIDE_MASKS)
    shape = (adjoint.shape[0], half)
    depth = operator.shape[0]
    up_keep, up_send, adj = half_products(
        functools.partial(upper_kernel, blocks, order),
        blocks,
        operator,
        pieces,
        shape,
        (jax.ShapeDtypeStruct((shape[0], depth), adjoint.dtype),),
        (pltpu.VMEM((depth, 128), F32),),
    )
    slots = (blocks // 2, blocks * CAP, 128)
    far_keep, far_send, near_slots = half_products(
        functools.partial(far_kernel, blocks, slot_order),
        blocks // 2,
        operator,
        code_pieces + [up_keep, up_send, adj],
        shape,
        (jax.ShapeDtypeStruct(slots, BF16),),
        (pltpu.VMEM(slots, BF16),),
        more=1,
    )
    near_keep, near_send = half_products(
        functools.partial(near_kernel, blocks), blocks // 2, operator, [near_slots, adj], shape
    )
    upper = up_keep + swap(up_send, "wide", 1)
    far_in = swap(far_send, "wide", 1)
    far = far_keep + far_in[:-1]
    level = jnp.maximum(far_send[-1, 0:1], far_in[-1, 0:1]) + 1.0
    near = near_keep + swap(near_send, "wide", 1)
    far = jnp.stack([far, upper[4:]], axis=1)
    near = jnp.stack([near, upper[:4]], axis=1)
    message = swap(pack(far[2:4], level), "wide", 6)
    r2, other = unpack(message, far[2:4].shape)
    level = jnp.maximum(level, other) + 1.0
    message = swap(pack(far[1] + r2[0], level), "wide", 2)
    t2, other = unpack(message, far[1].shape)
    level = jnp.maximum(level, other) + 1.0
    message = swap(pack(far[0] + r2[1] + t2, level), "wide", 8)
    across, other = unpack(message, far[0].shape)
    r1 = swap(near[2:4], "wide", 6)
    t1 = swap(near[1] + r1[0], "wide", 2)
    total = near[0] + r1[1] + t1 + across
    return jnp.concatenate([total[0], jnp.where(code[0:1] >= 0, 0.0, total[1])], axis=1)


def solution(mesh):
    return jax.shard_map(
        program,
        mesh=mesh,
        in_specs=(P(None, ("wide", "col")), P("wide", "col"), P(("col", "wide"))),
        out_specs=P(None, ("col", "wide")),
        check_vma=False,
    )
```
